256 devices in a mesh: tok: 16 (over y, x), feat: 16 (over z, core).
Axes of the slice: x: 4, y: 4, z: 8, core: 2. Of those that a mesh axis runs over, the one named last changes fastest.
Arguments:
- calib: float32 [16384, 22016], P('tok', 'feat')
- teacher_w: bfloat16 [22016, 256], P('feat'), may hold values from -6 to 6
- mask: int32 [172, 2], replicated, may hold values from 0 to 1, as said below
Outputs:
- solution: float32 [22016, 256], P('feat')
- residual: float32 [22016, 256], P('feat')
The draws below stay inside these ranges and needn't reach their ends.
Inputs may be any that keep to these rules, and one draw needn't show every extreme that they name: `mask`: every column block has at least one row block with 1.
All inputs are finite; a program needn't handle non-finite values.
Results may differ from the reference program's by a relative error of at most 0.0003.
Values sent between devices are 32-bit elements; how exact they have to be, the bound alone decides.
No kernel may reach another device: no remote copies, remote signals or barrier semaphores. Data moves between devices by JAX's collectives and lax.ppermute only.
A program may use at most 64 MiB of HBM per device.

```python
import jax
import jax.numpy as jnp
from jax import lax

DIN = 22016
COLS = 256
BLOCK = 128
ITERS = 2
ROWS = 16384


def draw_calib(key, part):
    key_base, key_col, key_row = jax.random.split(key, 3)
    col_scale = jnp.exp(jax.random.uniform(key_col, (1, DIN), jnp.float32, jnp.log(0.3), jnp.log(3.0)))
    position = jnp.arange(ROWS, dtype=jnp.float32)[:, None] / ROWS
    base = jax.random.normal(key_base, (ROWS, DIN), jnp.float32)
    row_scale = jnp.exp(jax.random.uniform(key_row, (ROWS, 1), jnp.float32, jnp.log(0.5), jnp.log(2.0)))
    ramp = jnp.exp(0.5 * jnp.log(10.0) * position)
    return base * col_scale * row_scale * ramp * DIN ** (-0.5)


def draw_mask(key, part):
    key_base, key_pick = jax.random.split(jax.random.fold_in(key, 7))
    row_blocks = DIN // BLOCK
    col_blocks = COLS // BLOCK
    base = jax.random.randint(key_base, (row_blocks, col_blocks), 0, 2).astype(jnp.int32)
    picked = jax.random.randint(key_pick, (col_blocks,), 0, row_blocks).astype(jnp.int32)
    forced = (jnp.arange(row_blocks, dtype=jnp.int32)[:, None] == picked[None, :]).astype(jnp.int32)
    return jnp.maximum(base, forced)


def block_scale(rng, extent, shards, low, largest):
    gain = 1.0
    for axis_at, parts in shards:
        draws = jax.random.uniform(jax.random.fold_in(jax.random.fold_in(rng, 6), axis_at), (parts,), jnp.float32, low / len(shards), largest / len(shards))
        gain = gain * jnp.repeat(jnp.exp(draws), extent[axis_at] // parts).reshape((-1,) + (1,) * (len(extent) - 1 - axis_at))
    return gain


def normal_values(stream_key, shape, scale, bound, cuts=(), kind=jnp.bfloat16):
    array = scale * jax.random.normal(stream_key, shape, jnp.float32)
    if cuts:
        array = array * block_scale(stream_key, shape, cuts, -0.22, 0.18)
    return jnp.clip(array, -bound, bound).astype(kind)


def setup_inputs(seed: int = 0) -> dict:
    streams_of = jax.random.split(jax.random.key(seed), 4)
    calib = draw_calib(jax.random.fold_in(streams_of[3], 71), 0)
    teacher_w = normal_values(streams_of[1], (DIN, COLS), 1.0, 6.0, ((0, 16),))
    mask = draw_mask(jax.random.fold_in(streams_of[3], 71), 0)
    return dict(calib=calib, teacher_w=teacher_w, mask=mask)


DAMP_REL = 0.2


def reference(calib, teacher_w, mask):
    live = jnp.repeat(jnp.repeat(mask.astype(jnp.float32), BLOCK, axis=0), BLOCK, axis=1)
    damp = DAMP_REL * jnp.sum(calib * calib) / DIN

    def gram(vec):
        rows_out = jnp.dot(calib, vec, precision=lax.Precision.HIGHEST, preferred_element_type=jnp.float32)
        back = jnp.dot(calib.T, rows_out, precision=lax.Precision.HIGHEST, preferred_element_type=jnp.float32)
        return live * back

    targets = gram(teacher_w.astype(jnp.float32))
    solution = jnp.zeros_like(targets)
    residual = targets
    direction = targets
    norm_now = jnp.sum(residual * residual, axis=0)
    for step in range(ITERS):
        image = gram(direction) + damp * direction
        curvature = jnp.sum(direction * image, axis=0)
        alpha = norm_now / curvature
        solution = solution + alpha * direction
        residual = residual - alpha * image
        fresh = jnp.sum(residual * residual, axis=0)
        direction = residual + (fresh / norm_now) * direction
        norm_now = fresh
    return solution, residual
```

```python
import jax
import jax.numpy as jnp
from jax import lax
from jax.experimental import pallas as pl
from jax.experimental.pallas import tpu as pltpu
from jax.sharding import PartitionSpec as P

BLOCK = 128
DAMP_REL = 0.2
SPARE = 8
RING = 8
SIDE = 4


def split(values):
    high = lax.reduce_precision(values, 8, 7)
    return high.astype(jnp.bfloat16), (values - high).astype(jnp.bfloat16)


def product(pair, right, contract):
    def dot(a, b):
        dims = (((contract,), (0,)), ((), ()))
        return lax.dot_general(a, b, dims, preferred_element_type=jnp.float32)

    high, low = pair
    if not isinstance(right[0], tuple):
        both = jnp.concatenate(right, axis=1)
        out = dot(high, both) + dot(low, both)
        width = out.shape[1] // 2
        return out[:, :width], out[:, width:]
    width = right[0][0].shape[1]
    cross = dot(low, jnp.concatenate([right[0][0], right[1][0]], axis=1))
    outs = []
    for i in range(2):
        wide = dot(high, jnp.concatenate(right[i], axis=1))
        outs.append(wide[:, :width] + (wide[:, width:] + cross[:, i * width : (i + 1) * width]))
    return tuple(outs)


def prepare_kernel(order_ref, calib_ref, near_ref, *outs):
    own_high, own_low, other_high, other_low, squares_ref = outs
    step = pl.program_id(0)

    def put(values, high_ref, low_ref):
        high = values.astype(jnp.bfloat16)
        high_ref[...] = high
        low_ref[...] = (values - high.astype(jnp.float32)).astype(jnp.bfloat16)
        squares = values * values
        squares_ref[...] += jnp.sum(squares.reshape(-1, 8, squares.shape[1]), axis=0)

    def paired(first):
        far, near = calib_ref[...], near_ref[...]
        piece = far.shape[1] // 2
        lane = lax.broadcasted_iota(jnp.int32, far.shape, 1)
        lows = jnp.where(lane < piece, far, pltpu.roll(near, piece, 1))
        highs = jnp.where(lane < piece, pltpu.roll(far, piece, 1), near)
        return jnp.where(first, lows, highs)

    @pl.when(step == 0)
    def _():
        squares_ref[...] = jnp.zeros_like(squares_ref)

    @pl.when(step < 3)
    def _():
        put(calib_ref[...], own_high, own_low)

    @pl.when(step == 3)
    def _():
        put(paired(order_ref[9] == 0), own_high, own_low)

    @pl.when((step > 3) & (step < 7))
    def _():
        put(calib_ref[...], other_high, other_low)

    @pl.when(step == 7)
    def _():
        put(paired(order_ref[9] != 0), other_high, other_low)


def prepare(calib_t, order):
    width, rows = calib_t.shape
    chunk = rows // RING
    half = jax.ShapeDtypeStruct((width, rows // 2), jnp.bfloat16)
    own = pl.BlockSpec((width, chunk), lambda i, order: (0, jnp.minimum(i, 3)))
    other = pl.BlockSpec((width, chunk), lambda i, order: (0, jnp.maximum(i, 4) - 4))
    return pl.pallas_call(
        prepare_kernel,
        grid_spec=pltpu.PrefetchScalarGridSpec(
            num_scalar_prefetch=1,
            grid=(RING,),
            in_specs=[
                pl.BlockSpec((width, chunk), lambda i, order: (0, order[i])),
                pl.BlockSpec((width, chunk), lambda i, order: (0, order[8])),
            ],
            out_specs=[own, own, other, other, pl.BlockSpec((8, chunk), lambda i, order: (0, 0))],
        ),
        out_shape=[half, half, half, half, jax.ShapeDtypeStruct((8, chunk), jnp.float32)],
        compiler_params=pltpu.CompilerParams(vmem_limit_bytes=24 * 2**20),
    )(order, calib_t, calib_t)


def on_device(calib, teacher_w, mask):
    feat_count = lax.axis_size("feat")
    tok_count = lax.axis_size("tok")
    feat_place = lax.axis_index("feat")
    tok_place = lax.axis_index("tok")
    core = feat_place % 2
    ring_place = feat_place // 2
    side_place = jnp.where(core == 0, tok_place % SIDE, tok_place // SIDE)
    rows_dev, din_dev = calib.shape
    cols = teacher_w.shape[1]
    wide = cols // 2
    chunk = rows_dev // RING
    piece = chunk // 2
    quarter = din_dev // 2

    core_swap = [(i, i ^ 1) for i in range(feat_count)]

    def ring_shift(d):
        return [
            (2 * z + c, 2 * ((z + (d if c == 0 else -d)) % RING) + c)
            for z in range(RING)
            for c in range(2)
        ]

    def side_shift(d, first):
        pairs = []
        for y in range(SIDE):
            for x in range(SIDE):
                for z in range(RING):
                    for c in range(2):
                        along_x = (c == 0) == first
                        to_x = (x + d) % SIDE if along_x else x
                        to_y = y if along_x else (y + d) % SIDE
                        feat = 2 * z + c
                        pairs.append(
                            ((y * SIDE + x) * feat_count + feat, (to_y * SIDE + to_x) * feat_count + feat)
                        )
        return pairs

    def exchange(values):
        return lax.ppermute(values, "feat", core_swap)

    def ring(values, d):
        return lax.ppermute(values, "feat", ring_shift(d))

    def side(values, d, first):
        return lax.ppermute(values, ("tok", "feat"), side_shift(d % SIDE, first))

    sign = 1 - 2 * core
    far_place = (ring_place + RING // 2) % RING
    ahead = [(ring_place + sign * d + RING) % RING for d in (1, 2, 3)]
    behind = [(ring_place - sign * d + RING) % RING for d in (1, 2, 3)]
    order = jnp.stack(ahead + [far_place] + behind + [far_place, ring_place, core])
    own_high, own_low, other_high, other_low, squares = prepare(calib.T, order.astype(jnp.int32))
    own, other = (own_high, own_low), (other_high, other_low)
    squares = jnp.sum(squares)

    first_row = feat_place * din_dev
    block_ids = (first_row + jnp.arange(din_dev, dtype=jnp.int32)) // BLOCK
    onehot = block_ids[:, None] == jnp.arange(mask.shape[0], dtype=jnp.int32)[None, :]
    mask_pair = jnp.where(core == 0, mask, mask[:, ::-1])
    live_all = jnp.dot(
        onehot.astype(jnp.bfloat16),
        jnp.repeat(mask_pair.astype(jnp.bfloat16), BLOCK, axis=1),
        preferred_element_type=jnp.float32,
    )
    live = (live_all[:, :wide], live_all[:, wide:])

    def join(pair):
        return jnp.concatenate(pair, axis=1)

    def forward(right, extras):
        sent = product(other, right, 0)[::-1]
        kept = join(product(own, right, 0))
        half = kept.shape[0]
        if extras is None:
            kept = kept + exchange(join(sent))
        else:
            got = exchange(jnp.concatenate([join(sent), join(extras[::-1])], axis=0))
            kept = kept + got[:half]
            extras = join(extras) + got[half:]

        def message(d):
            part = kept[(d - 1) * chunk : d * chunk] if d < 4 else kept[3 * chunk : 3 * chunk + piece]
            if extras is None:
                return part
            return jnp.concatenate([part, extras], axis=0)

        got = {d: ring(message(d), d) for d in (4, 3, 2, 1)}
        near = got[1] + (got[2] + got[3])
        mine = got[4][:piece] + kept[3 * chunk + piece :]
        nothing = jnp.zeros_like(mine)
        mine = jnp.where(
            core == 0, jnp.concatenate([mine, nothing]), jnp.concatenate([nothing, mine])
        )
        part = near[:chunk] + mine
        if extras is not None:
            totals = near[chunk:] + jnp.where(core == 0, got[4][piece:] + extras, 0.0)
            part = jnp.concatenate([part, totals], axis=0)
        swapped = exchange(jnp.concatenate([part[:, wide:], part[:, :wide]], axis=1))
        total = part + swapped
        block = total[:chunk]
        far = jnp.where(core == 0, block[piece:], block[:piece])
        got = [ring(far, 4)] + [ring(block, d) for d in (3, 2, 1)]
        rows_other = jnp.concatenate([got[3], got[2], got[1], got[0], far], axis=0)
        rows_own = exchange(jnp.concatenate([rows_other[:, wide:], rows_other[:, :wide]], axis=1))
        return rows_own, rows_other, total[chunk:]

    def pairwise(here, before, after, across):
        return (here + across) + (before + after)

    def backward(rows_own, rows_other, extras):
        rights = [(split(rows[:, :wide]), split(rows[:, wide:])) for rows in (rows_other, rows_own)]
        first, second = product(other, rights[0], 1), product(own, rights[1], 1)
        got = exchange(first[1] + second[1])
        mine = first[0] + second[0]
        quarters = jnp.stack([mine[:quarter], mine[quarter:], got[:quarter], got[quarter:]])

        def at(d):
            place = (side_place + d) % SIDE
            part = lax.dynamic_index_in_dim(quarters, place, 0, keepdims=False)
            return jnp.concatenate([part, extras], axis=0)

        across = side(at(2), 2, True)
        before, after = side(at(1), 1, True), side(at(3), 3, True)
        summed = pairwise(at(0), before, after, across)
        across = side(summed, 2, False)
        before, after = side(summed, 1, False), side(summed, 3, False)
        summed = pairwise(summed, before, after, across)
        block, totals = summed[:quarter], summed[quarter:]
        full = jnp.zeros((SIDE, quarter, wide), jnp.float32)
        full = lax.dynamic_update_index_in_dim(full, block, side_place, 0)
        for d in (2, 1, 3):
            place = (side_place - d + SIDE) % SIDE
            full = lax.dynamic_update_index_in_dim(full, side(block, d, True), place, 0)
        full = full.reshape(SIDE * quarter, wide)
        got = exchange(jnp.concatenate([full[din_dev:], totals], axis=0))
        return (full[:din_dev], got[:din_dev]), (totals, got[din_dev:])

    def lines(*values):
        width = values[0].shape[0]
        fill = jnp.zeros((SPARE - len(values), width), jnp.float32)
        return jnp.concatenate([jnp.stack(values), fill], axis=0)

    def each(function, *pairs):
        return tuple(function(*group) for group in zip(*pairs))

    def energy(rows_own, rows_other):
        rows_own, rows_other = rows_own[:, :wide], rows_other[:, :wide]
        return jnp.sum(rows_own * rows_own, axis=0) + jnp.sum(rows_other * rows_other, axis=0)

    def halves(line):
        return line[:wide], line[wide:]

    def dot_cols(a, b):
        return jnp.sum(a * b, axis=0)

    start = core * wide
    teacher = (
        lax.dynamic_slice_in_dim(teacher_w, start, wide, 1),
        lax.dynamic_slice_in_dim(teacher_w, wide - start, wide, 1),
    )
    rows_own, rows_other, unused = forward(teacher, None)
    summed, tail = backward(rows_own, rows_other, lines(jnp.full((wide,), squares)))
    targets = each(lambda l, s: l * s, live, summed)
    norm = each(dot_cols, targets, targets)
    own_0, other_0, totals = forward(
        each(split, targets), each(lambda n: lines(n, tail[0][0]), norm)
    )
    norm = halves(totals[0])
    damp = DAMP_REL * totals[1, 0] / (din_dev * feat_count)
    summed, tail = backward(own_0, other_0, lines(energy(own_0, other_0)))
    alpha = each(lambda n, t: n / (t[0] + damp * n), norm, tail)
    residual = each(
        lambda t, a, l, s: t - a * (l * s + damp * t), targets, alpha, live, summed
    )
    fresh = each(dot_cols, residual, residual)
    mixed = each(dot_cols, residual, targets)
    own_1, other_1, totals = forward(each(split, residual), each(lines, fresh, mixed))
    fresh, mixed = halves(totals[0]), halves(totals[1])
    beta = each(lambda f, n: f / n, fresh, norm)
    beta_row = jnp.concatenate(beta)
    own_1 = own_1 + beta_row * own_0
    other_1 = other_1 + beta_row * other_0
    direction = each(lambda r, b, t: r + b * t, residual, beta, targets)
    direction_norm = each(lambda f, b, m, n: f + b * (2.0 * m + b * n), fresh, beta, mixed, norm)
    summed, tail = backward(own_1, other_1, lines(energy(own_1, other_1)))
    step = each(lambda f, t, n: f / (t[0] + damp * n), fresh, tail, direction_norm)
    result = each(lambda a, t, s, d: a * t + s * d, alpha, targets, step, direction)
    residual = each(
        lambda r, a, l, s, d: r - a * (l * s + damp * d), residual, step, live, summed, direction
    )

    def ordered(pair):
        return jnp.where(core == 0, join(pair), join(pair[::-1]))

    return ordered(result), ordered(residual)


def solution(mesh):
    in_specs = (P("tok", "feat"), P("feat", None), P())
    out_specs = (P("feat", None), P("feat", None))
    return jax.shard_map(
        on_device, mesh=mesh, in_specs=in_specs, out_specs=out_specs, check_vma=False
    )
```

```python
import jax
import jax.numpy as jnp
from jax import lax
from jax.experimental import pallas as pl
from jax.experimental.pallas import tpu as pltpu
from jax.sharding import PartitionSpec as P

BLOCK = 128
DAMP_REL = 0.2
SPARE = 8
RING = 8
SIDE = 4
PARTS = 1


def split(values):
    high = lax.reduce_precision(values, 8, 7)
    return high.astype(jnp.bfloat16), (values - high).astype(jnp.bfloat16)


def dot(left, right, contract):
    dims = (((contract,), (0,)), ((), ()))
    return lax.dot_general(left, right, dims, preferred_element_type=jnp.float32)


def product(pair, right):
    high, low = pair
    if not isinstance(right[0], tuple):
        both = jnp.concatenate(right, axis=1)
        out = dot(high, both, 0) + dot(low, both, 0)
        width = out.shape[1] // 2
        return out[:, :width], out[:, width:]
    width = right[0][0].shape[1]
    cross = dot(low, jnp.concatenate([right[0][0], right[1][0]], axis=1), 0)
    outs = []
    for i in range(2):
        wide = dot(high, jnp.concatenate(right[i], axis=1), 0)
        outs.append(wide[:, :width] + (wide[:, width:] + cross[:, i * width : (i + 1) * width]))
    return tuple(outs)


def prepare_kernel(order_ref, calib_ref, near_ref, *outs):
    own_high, own_low, other_high, other_low, squares_ref = outs
    step = pl.program_id(0)

    def put(values, high_ref, low_ref):
        high = values.astype(jnp.bfloat16)
        high_ref[...] = high
        low_ref[...] = (values - high.astype(jnp.float32)).astype(jnp.bfloat16)
        squares = values * values
        squares_ref[...] += jnp.sum(squares.reshape(-1, 8, squares.shape[1]), axis=0)

    def paired(first):
        far, near = calib_ref[...], near_ref[...]
        piece = far.shape[1] // 2
        lane = lax.broadcasted_iota(jnp.int32, far.shape, 1)
        lows = jnp.where(lane < piece, far, pltpu.roll(near, piece, 1))
        highs = jnp.where(lane < piece, pltpu.roll(far, piece, 1), near)
        return jnp.where(first, lows, highs)

    @pl.when(step == 0)
    def _():
        squares_ref[...] = jnp.zeros_like(squares_ref)

    @pl.when(step < 3)
    def _():
        put(calib_ref[...], own_high, own_low)

    @pl.when(step == 3)
    def _():
        put(paired(order_ref[9] == 0), own_high, own_low)

    @pl.when((step > 3) & (step < 7))
    def _():
        put(calib_ref[...], other_high, other_low)

    @pl.when(step == 7)
    def _():
        put(paired(order_ref[9] != 0), other_high, other_low)
        total = jnp.sum(jnp.sum(squares_ref[...], axis=0, keepdims=True), axis=1, keepdims=True)
        squares_ref[...] = jnp.broadcast_to(total, squares_ref.shape)


def prepare(calib_t, order):
    width, rows = calib_t.shape
    chunk = rows // RING
    half = jax.ShapeDtypeStruct((width, rows // 2), jnp.bfloat16)
    own = pl.BlockSpec((width, chunk), lambda i, order: (0, jnp.minimum(i, 3)))
    other = pl.BlockSpec((width, chunk), lambda i, order: (0, jnp.maximum(i, 4) - 4))
    return pl.pallas_call(
        prepare_kernel,
        grid_spec=pltpu.PrefetchScalarGridSpec(
            num_scalar_prefetch=1,
            grid=(RING,),
            in_specs=[
                pl.BlockSpec((width, chunk), lambda i, order: (0, order[i])),
                pl.BlockSpec((width, chunk), lambda i, order: (0, order[8])),
            ],
            out_specs=[own, own, other, other, pl.BlockSpec((8, chunk), lambda i, order: (0, 0))],
        ),
        out_shape=[half, half, half, half, jax.ShapeDtypeStruct((8, chunk), jnp.float32)],
        compiler_params=pltpu.CompilerParams(vmem_limit_bytes=24 * 2**20),
    )(order, calib_t, calib_t)


def on_device(calib, teacher_w, mask):
    feat_count = lax.axis_size("feat")
    tok_count = lax.axis_size("tok")
    feat_place = lax.axis_index("feat")
    tok_place = lax.axis_index("tok")
    core = feat_place % 2
    ring_place = feat_place // 2
    side_place = jnp.where(core == 0, tok_place % SIDE, tok_place // SIDE)
    rows_dev, din_dev = calib.shape
    cols = teacher_w.shape[1]
    wide = cols // 2
    chunk = rows_dev // RING
    piece = chunk // 2
    quarter = din_dev // 2

    core_swap = [(i, i ^ 1) for i in range(feat_count)]

    def ring_shift(d):
        return [
            (2 * z + c, 2 * ((z + (d if c == 0 else -d)) % RING) + c)
            for z in range(RING)
            for c in range(2)
        ]

    def side_shift(d, first):
        pairs = []
        for y in range(SIDE):
            for x in range(SIDE):
                for z in range(RING):
                    for c in range(2):
                        along_x = (c == 0) == first
                        to_x = (x + d) % SIDE if along_x else x
                        to_y = y if along_x else (y + d) % SIDE
                        feat = 2 * z + c
                        pairs.append(
                            ((y * SIDE + x) * feat_count + feat, (to_y * SIDE + to_x) * feat_count + feat)
                        )
        return pairs

    def exchange(values):
        return lax.ppermute(values, "feat", core_swap)

    def ring(values, d):
        return lax.ppermute(values, "feat", ring_shift(d))

    def side(values, d, first):
        return lax.ppermute(values, ("tok", "feat"), side_shift(d % SIDE, first))

    first_row = feat_place * din_dev
    block_ids = (first_row + jnp.arange(din_dev, dtype=jnp.int32)) // BLOCK
    onehot = block_ids[:, None] == jnp.arange(mask.shape[0], dtype=jnp.int32)[None, :]
    leading = (jnp.arange(cols, dtype=jnp.int32) < wide) == (core == 0)
    mask_pair = jnp.where(leading[None, :], mask[:, :1], mask[:, 1:]).astype(jnp.bfloat16)
    live_all = jnp.dot(onehot.astype(jnp.bfloat16), mask_pair, preferred_element_type=jnp.float32)
    start = core * wide
    teacher = (
        lax.dynamic_slice_in_dim(teacher_w, start, wide, 1),
        lax.dynamic_slice_in_dim(teacher_w, wide - start, wide, 1),
    )

    sign = 1 - 2 * core
    far_place = (ring_place + RING // 2) % RING
    ahead = [(ring_place + sign * d + RING) % RING for d in (1, 2, 3)]
    behind = [(ring_place - sign * d + RING) % RING for d in (1, 2, 3)]
    order = jnp.stack(ahead + [far_place] + behind + [far_place, ring_place, core])
    order, live_all, *teacher = lax.optimization_barrier((order, live_all, *teacher))
    own_high, own_low, other_high, other_low, squares = prepare(calib.T, order.astype(jnp.int32))
    own, other = (own_high, own_low), (other_high, other_low)
    live = (live_all[:, :wide], live_all[:, wide:])

    def join(pair):
        return jnp.concatenate(pair, axis=1)

    def forward(right, extras):
        sent = product(other, right)[::-1]
        kept = join(product(own, right))
        half = kept.shape[0]
        if extras is None:
            kept = kept + exchange(join(sent))
        else:
            got = exchange(jnp.concatenate([join(sent), join(extras[::-1])], axis=0))
            kept = kept + got[:half]
            extras = join(extras) + got[half:]

        def message(d):
            part = kept[(d - 1) * chunk : d * chunk] if d < 4 else kept[3 * chunk : 3 * chunk + piece]
            if extras is None:
                return part
            return jnp.concatenate([part, extras], axis=0)

        got = {d: ring(message(d), d) for d in (4, 3, 2, 1)}
        near = got[1] + (got[2] + got[3])
        mine = got[4][:piece] + kept[3 * chunk + piece :]
        nothing = jnp.zeros_like(mine)
        mine = jnp.where(
            core == 0, jnp.concatenate([mine, nothing]), jnp.concatenate([nothing, mine])
        )
        part = near[:chunk] + mine
        if extras is not None:
            totals = near[chunk:] + jnp.where(core == 0, got[4][piece:] + extras, 0.0)
            part = jnp.concatenate([part, totals], axis=0)
        swapped = exchange(jnp.concatenate([part[:, wide:], part[:, :wide]], axis=1))
        total = part + swapped
        block = total[:chunk]
        far = jnp.where(core == 0, block[piece:], block[:piece])
        got = [ring(far, 4)] + [ring(block, d) for d in (3, 2, 1)]
        rows_other = jnp.concatenate([got[3], got[2], got[1], got[0], far], axis=0)
        rows_own = exchange(jnp.concatenate([rows_other[:, wide:], rows_other[:, :wide]], axis=1))
        return rows_own, rows_other, total[chunk:]

    def pairwise(here, before, after, across):
        return (here + across) + (before + after)

    def backward(rows_own, rows_other, extras):
        pairs = [(other, rows_other), (own, rows_own)]
        terms = [(split(rows[:, :wide]), split(rows[:, wide:])) for _, rows in pairs]
        cross = sum(
            dot(low, join((mine[0], their[0])), 1) for ((_, low), _), (mine, their) in zip(pairs, terms)
        )
        part = sum(dot(high, join(their), 1) for ((high, _), _), (_, their) in zip(pairs, terms))
        theirs = part[:, :wide] + (part[:, wide:] + cross[:, wide:])
        got = exchange(theirs)
        ready = [join(mine) for mine, _ in terms]
        *ready, _ = lax.optimization_barrier((*ready, theirs))
        part = sum(dot(high, right, 1) for ((high, _), _), right in zip(pairs, ready))
        mine = part[:, :wide] + (part[:, wide:] + cross[:, :wide])
        quarters = jnp.stack([mine[:quarter], mine[quarter:], got[:quarter], got[quarter:]])

        depth = quarter // PARTS
        summed, totals, totals_their = [], None, None

        def reduce(at, first):
            across = side(at(2), 2, first)
            before, after = side(at(1), 1, first), side(at(3), 3, first)
            return pairwise(at(0), before, after, across)

        firsts = []
        for i in range(PARTS):

            def at(d, i=i):
                place = (side_place + d) % SIDE
                start = (place, i * depth, 0)
                part = lax.dynamic_slice(quarters, start, (1, depth, wide))[0]
                return part if i else jnp.concatenate([part, extras], axis=0)

            firsts.append(reduce(at, True))
        for i in range(PARTS):
            summed.append(reduce(lambda d, i=i: firsts[i], False))
        totals = summed[0][depth:]
        totals_their = exchange(totals)
        full = jnp.zeros((SIDE, quarter, wide), jnp.float32)
        for i in range(PARTS):
            block = summed[i][:depth]
            for d in (0, 2, 1, 3):
                place = (side_place - d + SIDE) % SIDE
                moved = side(block, d, True) if d else block
                full = lax.dynamic_update_slice(full, moved[None], (place, i * depth, 0))
        full = full.reshape(SIDE * quarter, wide)
        return (full[:din_dev], exchange(full[din_dev:])), (totals, totals_their)

    def lines(*values):
        width = values[0].shape[0]
        fill = jnp.zeros((SPARE - len(values), width), jnp.float32)
        return jnp.concatenate([jnp.stack(values), fill], axis=0)

    def each(function, *pairs):
        return tuple(function(*group) for group in zip(*pairs))

    def energy(rows_own, rows_other):
        rows_own, rows_other = rows_own[:, :wide], rows_other[:, :wide]
        return jnp.sum(rows_own * rows_own, axis=0) + jnp.sum(rows_other * rows_other, axis=0)

    def halves(line):
        return line[:wide], line[wide:]

    def dot_cols(a, b):
        return jnp.sum(a * b, axis=0)

    rows_own, rows_other, unused = forward(teacher, None)
    summed, tail = backward(rows_own, rows_other, squares)
    targets = each(lambda l, s: l * s, live, summed)
    norm = each(dot_cols, targets, targets)
    own_0, other_0, totals = forward(
        each(split, targets), each(lambda n: lines(n, tail[0][0]), norm)
    )
    norm = halves(totals[0])
    damp = halves(DAMP_REL / (din_dev * feat_count) * totals[1])
    summed, tail = backward(own_0, other_0, lines(energy(own_0, other_0)))
    alpha = each(lambda n, t, c: n / (t[0] + c * n), norm, tail, damp)
    residual = each(
        lambda t, a, l, s, c: t - a * (l * s + c * t), targets, alpha, live, summed, damp
    )
    fresh = each(dot_cols, residual, residual)
    mixed = each(dot_cols, residual, targets)
    own_1, other_1, totals = forward(each(split, residual), each(lines, fresh, mixed))
    fresh, mixed = halves(totals[0]), halves(totals[1])
    beta = each(lambda f, n: f / n, fresh, norm)
    beta_row = jnp.concatenate(beta)
    own_1 = own_1 + beta_row * own_0
    other_1 = other_1 + beta_row * other_0
    direction = each(lambda r, b, t: r + b * t, residual, beta, targets)
    direction_norm = each(lambda f, b, m, n: f + b * (2.0 * m + b * n), fresh, beta, mixed, norm)
    summed, tail = backward(own_1, other_1, lines(energy(own_1, other_1)))
    step = each(lambda f, t, n, c: f / (t[0] + c * n), fresh, tail, direction_norm, damp)
    result = each(lambda a, t, s, d: a * t + s * d, alpha, targets, step, direction)
    residual = each(
        lambda r, a, l, s, d, c: r - a * (l * s + c * d),
        residual,
        step,
        live,
        summed,
        direction,
        damp,
    )

    def ordered(pair):
        return jnp.where(core == 0, join(pair), join(pair[::-1]))

    return ordered(result), ordered(residual)


def solution(mesh):
    in_specs = (P("tok", "feat"), P("feat", None), P())
    out_specs = (P("feat", None), P("feat", None))
    return jax.shard_map(
        on_device, mesh=mesh, in_specs=in_specs, out_specs=out_specs, check_vma=False
    )
```
